256 devices in a mesh: dp: 32 (over z_lo, x, core), seq: 8 (over z_hi, y).
Axes of the slice: x: 4, y: 4, z: 8 (z_hi: 2, z_lo: 4; z = z_hi * 4 + z_lo), core: 2. Of those that a mesh axis runs over, the one named last changes fastest.
Arguments:
- tokens: bfloat16 [32, 3072, 1024], P('dp', 'seq'), may hold values from -6 to 6
- masks: int32 [32, 24, 24], P('dp', 'seq'), may hold values from 0 to 1, as said below
- ln_gain: float32 [1024], replicated, may hold values from 0.25 to 1.75
- ln_bias: float32 [1024], replicated, may hold values from -3 to 3
- w_qkv: bfloat16 [1024, 3072], P('dp'), may hold values from -0.4 to 0.4
- qkv_bias: float32 [3072], replicated, may hold values from -3 to 3
- w_out: bfloat16 [1024, 1024], P('dp'), may hold values from -0.1875 to 0.1875
- out_bias: float32 [1024], replicated, may hold values from -2 to 2
Outputs:
- updated: bfloat16 [32, 3072, 1024], P('dp', 'seq')
- context: bfloat16 [32, 3072, 1024], P('dp', 'seq')
The draws below stay inside these ranges and needn't reach their ends.
Inputs may be any that keep to these rules, and one draw needn't show every extreme that they name: Entries are 0 or 1; every diagonal entry masks[s, b, b] is 1.
All inputs are finite; a program needn't handle non-finite values.
Results may differ from the reference program's by a relative error of at most 0.012.
Values may be sent and summed in bfloat16 or wider, within the bound.
A program may use at most 192 MiB of HBM per device.

```python
import math
import jax
import jax.numpy as jnp
from jax import lax

D = 1024
HEADS = 16
BLOCK = 128
SEQLEN = 3072
SHEETS = 32
NB = 24


def draw_tokens(key, part):
    values = jnp.clip(jax.random.normal(jax.random.fold_in(key, 21), (SHEETS, SEQLEN, D), jnp.float32), -6.0, 6.0)
    return values.astype(jnp.bfloat16)


def draw_w_qkv(key, part):
    scaling = 2.0 / math.sqrt(D)
    values = jnp.clip(jax.random.normal(jax.random.fold_in(key, 31), (D, 3 * D), jnp.float32), -6.0, 6.0) * scaling
    values = jnp.clip(values, -0.398, 0.398)
    return values.astype(jnp.bfloat16)


def draw_masks(key, part):
    position = lax.iota(jnp.int32, NB)
    distance = jnp.minimum(position, NB - 1 - position)
    threshold = 5 + 180 * distance // NB
    occupied = jax.random.randint(jax.random.fold_in(key, 11), (SHEETS, NB), 0, 100) < threshold[None, :]
    kept = jax.random.randint(jax.random.fold_in(key, 12), (SHEETS, NB, NB), 0, 100) < 60
    pairs = occupied[:, :, None] & occupied[:, None, :] & kept
    diagonal = (position[:, None] == position[None, :])[None, :, :]
    return (pairs | diagonal).astype(jnp.int32)


def steps_of(stream_key, shape, shards, low, high):
    loudness = 1.0
    for dim, shards_of in shards:
        heights = jax.random.uniform(jax.random.fold_in(jax.random.fold_in(stream_key, 6), dim), (shards_of,), jnp.float32, low / len(shards), high / len(shards))
        loudness = loudness * jnp.repeat(jnp.exp(heights), shape[dim] // shards_of).reshape((-1,) + (1,) * (len(shape) - 1 - dim))
    return loudness


def scatter_about(own_key, shape, scale, most, shards=(), kind=jnp.bfloat16):
    loudness = steps_of(own_key, shape, shards, -0.22, 0.18) if shards else 1.0
    result = jax.random.normal(own_key, shape, jnp.float32) * scale * loudness
    return jnp.minimum(jnp.maximum(result, -most), most).astype(kind)


def setup_inputs(seed: int = 0) -> dict:
    key_of = jax.random.split(jax.random.key(seed), 9)
    return {
        "tokens": draw_tokens(jax.random.fold_in(key_of[8], 71), 0),
        "masks": draw_masks(jax.random.fold_in(key_of[8], 71), 0),
        "ln_gain": jnp.clip(1.0 + 0.15 * jax.random.normal(key_of[2], (D,), jnp.float32), 0.25, 1.75),
        "ln_bias": scatter_about(key_of[3], (D,), 0.5, 3.0, (), jnp.float32),
        "w_qkv": draw_w_qkv(jax.random.fold_in(key_of[8], 71), 0),
        "qkv_bias": scatter_about(key_of[5], (3 * D,), 0.5, 3.0, (), jnp.float32),
        "w_out": scatter_about(key_of[6], (D, D), D ** -0.5, 0.1875, ((0, 32),)),
        "out_bias": scatter_about(key_of[7], (D,), 0.3, 2.0, (), jnp.float32),
    }


NEG_FILL = -1e+30
EPSILON = 1e-06

def layer_norm(sheet, ln_gain, ln_bias):
    values = sheet.astype(jnp.float32)
    center = lax.optimization_barrier(jnp.mean(values, axis=-1, keepdims=True))
    spread = lax.optimization_barrier(jnp.mean(jnp.square(values - center), axis=-1, keepdims=True))
    normed = (values - center) * lax.rsqrt(spread + EPSILON)
    return (normed * ln_gain + ln_bias).astype(jnp.bfloat16)

def reference(tokens, masks, ln_gain, ln_bias, w_qkv, qkv_bias, w_out, out_bias):
    head_dim = D // HEADS
    scaling = head_dim ** (-0.5)

    def one_sheet(operands):
        sheet, mask_table = operands
        normed = layer_norm(sheet, ln_gain, ln_bias)
        packed = (jnp.dot(normed, w_qkv, preferred_element_type=jnp.float32) + qkv_bias).astype(jnp.bfloat16)
        queries = packed[:, :D].reshape(SEQLEN, HEADS, head_dim).transpose(1, 0, 2)
        keys_all = packed[:, D:2 * D].reshape(SEQLEN, HEADS, head_dim).transpose(1, 0, 2)
        values_all = packed[:, 2 * D:].reshape(SEQLEN, HEADS, head_dim).transpose(1, 0, 2)
        allowed = jnp.repeat(jnp.repeat(mask_table > 0, BLOCK, axis=0), BLOCK, axis=1)

        def one_head(triple):
            query_head, key_head, value_head = triple
            scores = jnp.dot(query_head, key_head.T, preferred_element_type=jnp.float32) * scaling
            masked = jnp.where(allowed, scores, NEG_FILL)
            row_top = lax.optimization_barrier(jnp.max(masked, axis=1, keepdims=True))
            weights = jnp.where(allowed, jnp.exp(scores - row_top), 0.0)
            totals = lax.optimization_barrier(jnp.sum(weights, axis=1, keepdims=True))
            mixed = jnp.dot(weights.astype(jnp.bfloat16), value_head, preferred_element_type=jnp.float32)
            return mixed / totals
        heads_out = lax.map(one_head, (queries, keys_all, values_all))
        context = heads_out.transpose(1, 0, 2).reshape(SEQLEN, D).astype(jnp.bfloat16)
        projected = jnp.dot(context, w_out, preferred_element_type=jnp.float32)
        updated = (sheet.astype(jnp.float32) + projected + out_bias).astype(jnp.bfloat16)
        return (updated, context)
    updated, context = lax.map(one_sheet, (tokens, masks))
    return (updated, context)
```

```python
import jax
import jax.numpy as jnp
from jax import lax
from jax.experimental import pallas as pl
from jax.experimental.pallas import tpu as pltpu
from jax.sharding import PartitionSpec as P

D = 1024
HEADS = 16
BLOCK = 128
NB = 24
STRIP = 384
STRIPS = 8
ROWS = 32
PAIRS = 8
CHUNKS = 4
CROWS = STRIP // CHUNKS
COLS = 512

NEG_FILL = -1e30
EPSILON = 1e-06
MESH = pl.DeviceIdType.MESH

SELF, BEFORE, AFTER, ACROSS = range(4)


def gather_kernel(tok_ref, gain_ref, beta_ref, wq_ref, bq_ref, wo_ref,
                  q_ref, k_hbm, v_hbm, wo_out,
                  toks, w_all, staged,
                  tsend, trecv, wsend, wrecv, ksem, vsem):
    dp = lax.axis_index("dp")
    sq = lax.axis_index("seq")
    core = lax.rem(dp, 2)
    x = lax.rem(dp // 2, 4)
    zl = dp // 8
    y = lax.rem(sq, 4)
    zh = sq // 4
    z = zh * 4 + zl

    def device(dx=0, dy=0, dz=0, flip=False):
        zz = lax.rem(z + dz + 8, 8)
        cc = 1 - core if flip else core
        return (lax.rem(zz, 4) * 8 + lax.rem(x + dx + 4, 4) * 2 + cc,
                (zz // 4) * 4 + lax.rem(y + dy + 4, 4))

    partners = [device(dx=1), device(dx=-1), device(dy=1), device(dy=-1), device(dz=1), device(dz=-1),
                device(dz=2), device(dz=-2), device(dz=4), device(flip=True)]
    barrier = pltpu.get_barrier_semaphore()
    for partner in partners:
        pl.semaphore_signal(barrier, inc=1, device_id=partner, device_id_type=MESH)
    pl.semaphore_wait(barrier, len(partners))

    def token_copy(plane, place, chunk):
        slot = plane * 4 + place
        if place == SELF:
            source, target = SELF, device(dz=4)
        elif place == BEFORE:
            source, target = plane * 4 + SELF, device(dy=1)
        elif place == AFTER:
            source, target = plane * 4 + SELF, device(dy=-1)
        elif chunk < CHUNKS // 2:
            source, target = plane * 4 + BEFORE, device(dy=1)
        else:
            source, target = plane * 4 + AFTER, device(dy=-1)
        rows = pl.ds(chunk * CROWS, CROWS)
        return pltpu.make_async_remote_copy(
            src_ref=toks.at[slot if False else source, rows], dst_ref=toks.at[slot, rows],
            send_sem=tsend.at[slot, chunk], recv_sem=trecv.at[slot, chunk],
            device_id=target, device_id_type=MESH)

    weights = (w_all, wo_out)

    def shard(k, dx, flip=False):
        zz = lax.rem(zl + (0, 3, 1, 2)[k], 4)
        cc = 1 - core if flip else core
        return zz * 8 + lax.rem(x + dx + 4, 4) * 2 + cc

    def weight_copy(which, name, k=0, place=SELF):
        ref = weights[which]
        first, count = 0, ROWS
        if name == "z":
            owner, index = shard(0, 0), k
            target = device(dz=(0, 1, -1, 2, -2)[k])
            if k >= 3:
                first, count = (k - 3) * (ROWS // 2), ROWS // 2
        elif name == "x":
            index = 5 + k * 4 + place
            if place == BEFORE:
                owner, target = shard(k, 0), device(dx=1)
            elif place == AFTER:
                owner, target = shard(k, 0), device(dx=-1)
            elif place == SELF:
                owner, target = shard(k, -1), device(dx=1)
                count = ROWS // 2
            else:
                owner, target = shard(k, 1), device(dx=-1)
                first, count = ROWS // 2, ROWS // 2
        else:
            index = 21 + k * 4 + place
            owner, target = shard(k, (0, -1, 1, 2)[place]), device(flip=True)
        rows = pl.ds(pl.multiple_of(owner * ROWS + first, ROWS // 2), count)
        return pltpu.make_async_remote_copy(
            src_ref=ref.at[rows], dst_ref=ref.at[rows],
            send_sem=wsend.at[which, index], recv_sem=wrecv.at[which, index],
            device_id=target, device_id_type=MESH)

    own_rows = pl.ds(pl.multiple_of(dp * ROWS, ROWS), ROWS)
    sent = []

    def go(copy):
        copy.start()
        sent.append(copy)

    w_all[own_rows, :] = wq_ref[...]
    wo_out[own_rows, :] = wo_ref[...]

    def spread(which, k):
        go(weight_copy(which, "x", k, BEFORE))
        go(weight_copy(which, "x", k, AFTER))
        go(weight_copy(which, "c", k, SELF))

    def around(which):
        for k in (1, 2, 3, 4):
            go(weight_copy(which, "z", k))
        spread(which, 0)

    def z_arrived(which, k):
        weight_copy(which, "z", k).wait_recv()
        if k == 3:
            weight_copy(which, "z", 4).wait_recv()
        spread(which, k)

    def x_arrived(which, k):
        weight_copy(which, "x", k, BEFORE).wait_recv()
        go(weight_copy(which, "x", k, SELF))
        go(weight_copy(which, "c", k, BEFORE))
        weight_copy(which, "x", k, AFTER).wait_recv()
        go(weight_copy(which, "x", k, ACROSS))
        go(weight_copy(which, "c", k, AFTER))

    def x_across(which, k):
        weight_copy(which, "x", k, SELF).wait_recv()
        weight_copy(which, "x", k, ACROSS).wait_recv()
        go(weight_copy(which, "c", k, ACROSS))

    def core_arrived(which):
        for k in range(4):
            for place in range(4):
                weight_copy(which, "c", k, place).wait_recv()

    def normalize(chunk):
        rows = pl.ds(chunk * CROWS, CROWS)
        values = tok_ref[rows, :].astype(jnp.float32)
        center = jnp.mean(values, axis=-1, keepdims=True)
        moved = values - center
        spread_ = jnp.mean(jnp.square(moved), axis=-1, keepdims=True)
        normed = moved * lax.rsqrt(spread_ + EPSILON)
        toks[SELF, rows, :] = (normed * gain_ref[...] + beta_ref[...]).astype(jnp.bfloat16)

    def offer(plane, chunk):
        go(token_copy(plane, BEFORE, chunk))
        go(token_copy(plane, AFTER, chunk))

    def pass_on(plane, chunk):
        token_copy(plane, BEFORE if chunk < CHUNKS // 2 else AFTER, chunk).wait_recv()
        go(token_copy(plane, ACROSS, chunk))

    def crossed(chunk):
        token_copy(1, SELF, chunk).wait_recv()
        offer(1, chunk)

    def rest(plane):
        for chunk in range(CHUNKS):
            token_copy(plane, AFTER if chunk < CHUNKS // 2 else BEFORE, chunk).wait_recv()

    def across(plane, chunks):
        for chunk in chunks:
            token_copy(plane, ACROSS, chunk).wait_recv()

    written = []

    def project(slot, first=0, count=STRIP):
        rows = slice(first, first + count)

        def body(n, _):
            cols = pl.ds(pl.multiple_of(D + n * COLS, COLS), COLS)
            made = jnp.dot(toks[slot, rows, :], w_all[:, cols], preferred_element_type=jnp.float32)
            staged[slot, rows, pl.ds(pl.multiple_of(n * COLS, COLS), COLS)] = (made + bq_ref[:, cols]).astype(jnp.bfloat16)
            return 0
        lax.fori_loop(0, 2 * D // COLS, body, 0)
        half = zh if slot < 4 else 1 - zh
        strip = half * 4 + lax.rem(y + (0, 3, 1, 2)[slot % 4], 4)
        there = pl.ds(pl.multiple_of(strip * STRIP + first, 64), count)
        part = 1 if first else 0
        for out, lane, sem in ((k_hbm, 0, ksem), (v_hbm, D, vsem)):
            copy = pltpu.make_async_copy(staged.at[slot, rows, lane:lane + D], out.at[there], sem.at[slot, part])
            copy.start()
            written.append(copy)

    around(0)
    for chunk in range(CHUNKS):
        normalize(chunk)
        offer(0, chunk)
        go(token_copy(1, SELF, chunk))
    z_arrived(0, 1)
    z_arrived(0, 2)
    pass_on(0, 0)
    x_arrived(0, 0)
    z_arrived(0, 3)
    pass_on(0, 1)
    crossed(0)
    x_arrived(0, 1)
    pass_on(0, 2)
    x_across(0, 0)
    x_arrived(0, 2)
    pass_on(0, 3)
    crossed(1)
    x_across(0, 1)
    x_arrived(0, 3)
    around(1)
    x_across(0, 2)
    x_across(0, 3)
    crossed(2)
    core_arrived(0)
    z_arrived(1, 1)
    z_arrived(1, 2)
    z_arrived(1, 3)

    def q_body(n, _):
        cols = pl.ds(pl.multiple_of(n * COLS, COLS), COLS)
        made = jnp.dot(toks[SELF], w_all[:, cols], preferred_element_type=jnp.float32)
        made = (made + bq_ref[:, cols]).astype(jnp.bfloat16)
        q_ref[:, cols] = made * jnp.bfloat16(0.125)
        return 0
    lax.fori_loop(0, D // COLS, q_body, 0)
    project(SELF)
    crossed(3)
    rest(0)
    pass_on(1, 0)
    pass_on(1, 1)
    project(BEFORE)
    x_arrived(1, 0)
    x_arrived(1, 1)
    project(AFTER)
    across(0, range(CHUNKS))
    x_arrived(1, 2)
    x_arrived(1, 3)
    pass_on(1, 2)
    project(ACROSS)
    pass_on(1, 3)
    project(4 + SELF)
    for k in range(4):
        x_across(1, k)
    rest(1)
    project(4 + BEFORE)
    project(4 + AFTER)
    half = CHUNKS // 2
    across(1, range(half))
    project(4 + ACROSS, 0, STRIP // 2)
    across(1, range(half, CHUNKS))
    project(4 + ACROSS, STRIP // 2, STRIP // 2)
    core_arrived(1)
    for copy in written:
        copy.wait()
    for copy in sent:
        copy.wait_send()


def gather(tokens, gain, beta, w_qkv, qkv_bias, w_out):
    vmem = pl.BlockSpec(memory_space=pltpu.VMEM)
    hbm = pl.BlockSpec(memory_space=pl.ANY)
    return pl.pallas_call(
        gather_kernel,
        name="gather_and_project",
        out_shape=(
            jax.ShapeDtypeStruct((STRIP, D), jnp.bfloat16),
            jax.ShapeDtypeStruct((STRIPS * STRIP, D), jnp.bfloat16),
            jax.ShapeDtypeStruct((STRIPS * STRIP, D), jnp.bfloat16),
            jax.ShapeDtypeStruct((D, D), jnp.bfloat16),
        ),
        in_specs=[vmem] * 6,
        out_specs=(vmem, hbm, hbm, vmem),
        scratch_shapes=[
            pltpu.VMEM((STRIPS, STRIP, D), jnp.bfloat16),
            pltpu.VMEM((D, 3 * D), jnp.bfloat16),
            pltpu.VMEM((STRIPS, STRIP, 2 * D), jnp.bfloat16),
            pltpu.SemaphoreType.DMA((STRIPS, CHUNKS)),
            pltpu.SemaphoreType.DMA((STRIPS, CHUNKS)),
            pltpu.SemaphoreType.DMA((2, 37)),
            pltpu.SemaphoreType.DMA((2, 37)),
            pltpu.SemaphoreType.DMA((STRIPS, 2)),
            pltpu.SemaphoreType.DMA((STRIPS, 2)),
        ],
        compiler_params=pltpu.CompilerParams(
            collective_id=0, has_side_effects=True, vmem_limit_bytes=44 * 2**20),
    )(tokens, gain, beta, w_qkv, qkv_bias, w_out)


def attend_kernel(m_ref, q_ref, k_hbm, v_hbm, tok_ref, wo_ref, bo_ref, upd_ref, ctx_ref,
                  idx, k_ref, v_ref, qz, s_scr, mx, lsum, acc, ksem, vsem):
    def fetch(hbm, ref, sem, j):
        rows = pl.ds(pl.multiple_of(j * BLOCK, BLOCK), BLOCK)
        return pltpu.make_async_copy(hbm.at[rows], ref.at[rows], sem.at[j])

    def each(hbm, ref, sem, start):
        def body(j, c):
            @pl.when(m_ref[0, j] + m_ref[1, j] + m_ref[2, j] > 0)
            def _():
                copy = fetch(hbm, ref, sem, j)
                if start:
                    copy.start()
                else:
                    copy.wait()
            return c
        lax.fori_loop(0, NB, body, 0)

    each(k_hbm, k_ref, ksem, True)
    each(v_hbm, v_ref, vsem, True)
    lane = lax.broadcasted_iota(jnp.int32, (BLOCK, 128), 1)
    low = lane < 64
    for i in range(STRIP // BLOCK):
        def build(j, c):
            idx[c] = j
            return c + (m_ref[i, j] > 0).astype(jnp.int32)
        n = lax.fori_loop(0, NB, build, jnp.int32(0))
        idx[n] = idx[n - 1]
        steps = (n + 1) // 2
        for hp in range(PAIRS):
            qv = q_ref[i * BLOCK:(i + 1) * BLOCK, hp * 128:(hp + 1) * 128]
            zero = jnp.zeros_like(qv)
            qz[hp, :BLOCK] = jnp.where(low, qv, zero)
            qz[hp, BLOCK:] = jnp.where(low, zero, qv)
        mx[...] = jnp.full_like(mx, NEG_FILL)
        lsum[...] = jnp.zeros_like(lsum)
        acc[...] = jnp.zeros_like(acc)
        if i == 0:
            each(k_hbm, k_ref, ksem, False)

        def pass1(t, _):
            r0 = pl.multiple_of(idx[2 * t] * BLOCK, BLOCK)
            r1 = pl.multiple_of(idx[2 * t + 1] * BLOCK, BLOCK)
            for hp in range(PAIRS):
                ln = slice(hp * 128, (hp + 1) * 128)
                kk = jnp.concatenate([k_ref[pl.ds(r0, BLOCK), ln], k_ref[pl.ds(r1, BLOCK), ln]], axis=0)
                s = lax.dot_general(qz[hp], kk, (((1,), (1,)), ((), ())), preferred_element_type=jnp.float32)
                s_scr[t, hp] = s
                mx[hp] = jnp.maximum(mx[hp], jnp.maximum(s[:, :128], s[:, 128:]))
            return 0
        lax.fori_loop(0, steps, pass1, 0)

        @pl.when(lax.rem(n, 2) == 1)
        def _():
            for hp in range(PAIRS):
                s_scr[steps - 1, hp, :, 128:] = jnp.full((256, 128), NEG_FILL, jnp.float32)
        for hp in range(PAIRS):
            mx[hp] = jnp.broadcast_to(jnp.max(mx[hp], axis=1, keepdims=True), (256, 128))
        if i == 0:
            each(v_hbm, v_ref, vsem, False)

        def pass2(t, _):
            r0 = pl.multiple_of(idx[2 * t] * BLOCK, BLOCK)
            r1 = pl.multiple_of(idx[2 * t + 1] * BLOCK, BLOCK)
            for hp in range(PAIRS):
                ln = slice(hp * 128, (hp + 1) * 128)
                s = s_scr[t, hp]
                mm = mx[hp]
                p0 = jnp.exp(s[:, :128] - mm)
                p1 = jnp.exp(s[:, 128:] - mm)
                lsum[hp] += p0 + p1
                pb = jnp.concatenate([p0.astype(jnp.bfloat16), p1.astype(jnp.bfloat16)], axis=1)
                vv = jnp.concatenate([v_ref[pl.ds(r0, BLOCK), ln], v_ref[pl.ds(r1, BLOCK), ln]], axis=0)
                acc[hp] += jnp.dot(pb, vv, preferred_element_type=jnp.float32)
            return 0
        lax.fori_loop(0, steps, pass2, 0)
        rows = slice(i * BLOCK, (i + 1) * BLOCK)
        for hp in range(PAIRS):
            o = acc[hp] / jnp.sum(lsum[hp], axis=1, keepdims=True)
            ctx_ref[rows, hp * 128:(hp + 1) * 128] = jnp.where(low, o[:BLOCK], o[BLOCK:]).astype(jnp.bfloat16)
        projected = jnp.dot(ctx_ref[rows], wo_ref[...], preferred_element_type=jnp.float32)
        upd_ref[rows] = (tok_ref[rows].astype(jnp.float32) + projected + bo_ref[...]).astype(jnp.bfloat16)


def attention(masks, q, k, v, tokens, w_out, out_bias):
    vmem = pl.BlockSpec(memory_space=pltpu.VMEM)
    hbm = pl.BlockSpec(memory_space=pl.ANY)
    return pl.pallas_call(
        attend_kernel,
        name="attend",
        out_shape=(jax.ShapeDtypeStruct((STRIP, D), jnp.bfloat16),) * 2,
        in_specs=[pl.BlockSpec(memory_space=pltpu.SMEM), vmem, hbm, hbm, vmem, vmem, vmem],
        out_specs=(vmem, vmem),
        scratch_shapes=[
            pltpu.SMEM((NB + 1,), jnp.int32),
            pltpu.VMEM((NB * BLOCK, D), jnp.bfloat16),
            pltpu.VMEM((NB * BLOCK, D), jnp.bfloat16),
            pltpu.VMEM((PAIRS, 256, 128), jnp.bfloat16),
            pltpu.VMEM((NB // 2, PAIRS, 256, 256), jnp.float32),
            pltpu.VMEM((PAIRS, 256, 128), jnp.float32),
            pltpu.VMEM((PAIRS, 256, 128), jnp.float32),
            pltpu.VMEM((PAIRS, 256, 128), jnp.float32),
            pltpu.SemaphoreType.DMA((NB,)),
            pltpu.SemaphoreType.DMA((NB,)),
        ],
        compiler_params=pltpu.CompilerParams(vmem_limit_bytes=58 * 2**20),
    )(masks, q, k, v, tokens, w_out, out_bias)


def on_device(tokens, masks, ln_gain, ln_bias, w_qkv, qkv_bias, w_out, out_bias):
    sheet = tokens[0]
    q, k, v, w_full = gather(sheet, ln_gain[None], ln_bias[None], w_qkv, qkv_bias[None], w_out)
    updated, context = attention(masks[0], q, k, v, sheet, w_full, out_bias[None])
    return (updated[None], context[None])


def solution(mesh):
    placed = (
        P("dp", "seq", None),
        P("dp", "seq", None),
        P(),
        P(),
        P("dp", None),
        P(),
        P("dp", None),
        P(),
    )
    return jax.shard_map(
        on_device,
        mesh=mesh,
        in_specs=placed,
        out_specs=(P("dp", "seq", None), P("dp", "seq", None)),
        check_vma=False,
    )
```

```python
import jax
import jax.numpy as jnp
from jax import lax
from jax.experimental import pallas as pl
from jax.experimental.pallas import tpu as pltpu
from jax.sharding import PartitionSpec as P

D = 1024
HEADS = 16
BLOCK = 128
NB = 24
STRIP = 384
STRIPS = 8
ROWS = 32
PAIRS = 8
CHUNKS = 8
AHEAD = 4
CROSSING = 2
CROWS = STRIP // CHUNKS

NEG_FILL = -1e30
EPSILON = 1e-06
MESH = pl.DeviceIdType.MESH

SELF, BEFORE, AFTER, ACROSS = range(4)


def gather_kernel(tok_hbm, gain_hbm, beta_hbm, wq_hbm, bq_hbm, wo_hbm,
                  q_hbm, k_hbm, v_hbm, wo_out,
                  tok_ref, gain_ref, beta_ref, bq_ref, toks, w_all, w_two, staged, q_ref,
                  tsend, trecv, wsend, wrecv, insem, ksem, vsem):
    dp = lax.axis_index("dp")
    sq = lax.axis_index("seq")
    core = lax.rem(dp, 2)
    x = lax.rem(dp // 2, 4)
    zl = dp // 8
    y = lax.rem(sq, 4)
    zh = sq // 4
    z = zh * 4 + zl

    def device(dx=0, dy=0, dz=0, flip=False):
        zz = lax.rem(z + dz + 8, 8)
        cc = 1 - core if flip else core
        return (lax.rem(zz, 4) * 8 + lax.rem(x + dx + 4, 4) * 2 + cc,
                (zz // 4) * 4 + lax.rem(y + dy + 4, 4))

    own_rows = pl.ds(pl.multiple_of(dp * ROWS, ROWS), ROWS)
    fills = [
        pltpu.make_async_copy(source, target, insem.at[i])
        for i, (source, target) in enumerate((
            (wq_hbm.at[:, D:], w_all.at[own_rows]), (tok_hbm, tok_ref), (wq_hbm.at[:, :D], w_two.at[own_rows, :D]),
            (wo_hbm, w_two.at[own_rows, D:]),
            (gain_hbm, gain_ref), (beta_hbm, beta_ref), (bq_hbm, bq_ref)))]
    for fill in fills:
        fill.start()

    partners = [device(dx=1), device(dx=-1), device(dy=1), device(dy=-1), device(dz=1), device(dz=-1),
                device(dz=2), device(dz=-2), device(dz=4), device(flip=True)]
    barrier = pltpu.get_barrier_semaphore()
    for partner in partners:
        pl.semaphore_signal(barrier, inc=1, device_id=partner, device_id_type=MESH)
    for fill in fills:
        fill.wait()
    pl.semaphore_wait(barrier, len(partners))

    def token_copy(plane, place, chunk):
        source = plane, SELF
        if place == SELF:
            source, target = (0, SELF), device(dz=4)
        elif place == BEFORE:
            target = device(dy=1)
        elif place == AFTER:
            target = device(dy=-1)
        elif chunk % 2 == 0:
            source, target = (plane, BEFORE), device(dy=1)
        else:
            source, target = (plane, AFTER), device(dy=-1)
        slot = plane * 4 + place
        return pltpu.make_async_remote_copy(
            src_ref=toks.at[source[0], chunk, source[1]], dst_ref=toks.at[plane, chunk, place],
            send_sem=tsend.at[slot, chunk], recv_sem=trecv.at[slot, chunk],
            device_id=target, device_id_type=MESH)

    weights = (w_all, w_two)

    def shard(k, dx):
        return lax.rem(zl + (0, 3, 1, 2)[k], 4) * 8 + lax.rem(x + dx + 4, 4) * 2 + core

    def weight_copy(which, name, k=0, place=SELF):
        ref = weights[which]
        first, count = 0, ROWS
        if name == "z":
            owner, index = shard(0, 0), k
            target = device(dz=(0, 1, -1, 2, -2)[k])
            if k >= 3:
                first, count = (k - 3) * (ROWS // 2), ROWS // 2
        elif name == "x":
            index = 5 + k * 4 + place
            if place == BEFORE:
                owner, target = shard(k, 0), device(dx=1)
            elif place == AFTER:
                owner, target = shard(k, 0), device(dx=-1)
            elif place == SELF:
                owner, target = shard(k, -1), device(dx=1)
                count = ROWS // 2
            else:
                owner, target = shard(k, 1), device(dx=-1)
                first, count = ROWS // 2, ROWS // 2
        else:
            index = 21 + k * 4 + place
            owner, target = shard(k, (0, -1, 1, 2)[place]), device(flip=True)
        rows = pl.ds(pl.multiple_of(owner * ROWS + first, ROWS // 2), count)
        return pltpu.make_async_remote_copy(
            src_ref=ref.at[rows], dst_ref=ref.at[rows],
            send_sem=wsend.at[which, index], recv_sem=wrecv.at[which, index],
            device_id=target, device_id_type=MESH)

    sent = []

    def go(copy):
        copy.start()
        sent.append(copy)

    def arrive(copy):
        copy.wait_recv()

    def spread(which, k):
        go(weight_copy(which, "x", k, BEFORE))
        go(weight_copy(which, "x", k, AFTER))
        go(weight_copy(which, "c", k, SELF))

    def around(which):
        for k in (1, 2, 3, 4):
            go(weight_copy(which, "z", k))

    def z_arrived(which, k):
        arrive(weight_copy(which, "z", k))
        if k == 3:
            arrive(weight_copy(which, "z", 4))
        spread(which, k)

    def x_arrived(which, k):
        arrive(weight_copy(which, "x", k, BEFORE))
        go(weight_copy(which, "x", k, SELF))
        go(weight_copy(which, "c", k, BEFORE))
        arrive(weight_copy(which, "x", k, AFTER))
        go(weight_copy(which, "x", k, ACROSS))
        go(weight_copy(which, "c", k, AFTER))

    def x_across(which, k):
        arrive(weight_copy(which, "x", k, SELF))
        arrive(weight_copy(which, "x", k, ACROSS))
        go(weight_copy(which, "c", k, ACROSS))

    def core_arrived(which):
        for k in range(4):
            for place in range(4):
                arrive(weight_copy(which, "c", k, place))

    def normalize(chunk):
        rows = pl.ds(chunk * CROWS, CROWS)
        values = tok_ref[rows, :].astype(jnp.float32)
        center = jnp.mean(values, axis=-1, keepdims=True)
        moved = values - center
        spread_ = jnp.mean(jnp.square(moved), axis=-1, keepdims=True)
        normed = moved * lax.rsqrt(spread_ + EPSILON)
        toks[0, chunk, SELF] = (normed * gain_ref[...] + beta_ref[...]).astype(jnp.bfloat16)

    def offer(plane, chunk):
        if chunk < CHUNKS:
            go(token_copy(plane, BEFORE, chunk))
            go(token_copy(plane, AFTER, chunk))

    def start():
        for chunk in range(CHUNKS):
            normalize(chunk)
            if chunk < AHEAD:
                offer(0, chunk)

    def cross(chunk):
        if chunk < CHUNKS:
            go(token_copy(1, SELF, chunk))

    def step(plane, chunk):
        first, second = (BEFORE, AFTER) if chunk % 2 == 0 else (AFTER, BEFORE)
        arrive(token_copy(plane, first, chunk))
        go(token_copy(plane, ACROSS, chunk))
        if plane == 0:
            offer(plane, chunk + AHEAD)
        arrive(token_copy(plane, second, chunk))

    def crossed(chunk):
        arrive(token_copy(1, SELF, chunk))
        cross(chunk + CROSSING)
        offer(1, chunk)

    def across(plane, chunks):
        for chunk in chunks:
            arrive(token_copy(plane, ACROSS, chunk))

    written = []

    def project(plane, first, end, piece):
        count = (end - first) * 4 * CROWS
        read = toks[plane, first:end].reshape(count, D)
        half = zh if plane == 0 else 1 - zh
        for lane, out, sem in ((0, k_hbm, ksem), (D, v_hbm, vsem)):
            made = jnp.dot(read, w_all[:, lane:D + lane], preferred_element_type=jnp.float32)
            made = (made + bq_ref[:, D + lane:2 * D + lane]).astype(jnp.bfloat16)
            staged[plane, first:end, :, :, lane:lane + D] = made.reshape(end - first, 4, CROWS, D)
            for place in range(4):
                strip = half * 4 + lax.rem(y + (0, 3, 1, 2)[place], 4)
                copy = pltpu.make_async_copy(
                    staged.at[plane, first:end, place, :, lane:lane + D], out.at[strip, first:end], sem.at[piece, place])
                copy.start()
                written.append(copy)

    def queries():
        own = toks[0, :, SELF].reshape(STRIP, D)
        made = jnp.dot(own, w_two[:, :D], preferred_element_type=jnp.float32)
        q_ref[...] = (made + bq_ref[:, :D]).astype(jnp.bfloat16) * jnp.bfloat16(0.125)
        copy = pltpu.make_async_copy(q_ref, q_hbm, insem.at[0])
        copy.start()
        written.append(copy)

    def output_weights():
        copy = pltpu.make_async_copy(w_two.at[:, D:], wo_out, insem.at[1])
        copy.start()
        written.append(copy)

    around(0)
    spread(0, 0)
    start()
    cross(0)
    step(0, 0)
    x_arrived(0, 0)
    step(0, 1)
    x_across(0, 0)
    z_arrived(0, 1)
    z_arrived(0, 2)
    z_arrived(0, 3)
    around(1)
    cross(1)
    step(0, 2)
    crossed(0)
    step(0, 3)
    step(0, 4)
    x_arrived(0, 1)
    x_arrived(0, 2)
    x_arrived(0, 3)
    spread(1, 0)
    step(0, 5)
    x_across(0, 1)
    x_across(0, 2)
    x_across(0, 3)
    z_arrived(1, 1)
    z_arrived(1, 2)
    z_arrived(1, 3)
    step(0, 6)
    crossed(1)
    core_arrived(0)
    x_arrived(1, 0)
    step(0, 7)
    across(0, range(CHUNKS))
    project(0, 0, 2, 0)
    crossed(2)
    step(1, 0)
    project(0, 2, 4, 1)
    x_arrived(1, 1)
    x_arrived(1, 2)
    x_arrived(1, 3)
    x_across(1, 0)
    crossed(3)
    step(1, 1)
    project(0, 4, 6, 2)
    crossed(4)
    step(1, 2)
    x_across(1, 1)
    x_across(1, 2)
    x_across(1, 3)
    project(0, 6, 8, 3)
    crossed(5)
    step(1, 3)
    across(1, (0, 1))
    project(1, 0, 2, 4)
    core_arrived(1)
    queries()
    crossed(6)
    step(1, 4)
    across(1, (2, 3))
    project(1, 2, 4, 5)
    crossed(7)
    step(1, 5)
    output_weights()
    step(1, 6)
    across(1, (4, 5))
    project(1, 4, 6, 6)
    step(1, 7)
    across(1, (6, 7))
    project(1, 6, 8, 7)
    for copy in written:
        copy.wait()
    for copy in sent:
        copy.wait_send()


def gather(tokens, gain, beta, w_qkv, qkv_bias, w_out):
    hbm = pl.BlockSpec(memory_space=pltpu.HBM)
    return pl.pallas_call(
        gather_kernel,
        name="gather_and_project",
        out_shape=(
            jax.ShapeDtypeStruct((STRIP, D), jnp.bfloat16),
            jax.ShapeDtypeStruct((STRIPS, CHUNKS, CROWS, D), jnp.bfloat16),
            jax.ShapeDtypeStruct((STRIPS, CHUNKS, CROWS, D), jnp.bfloat16),
            jax.ShapeDtypeStruct((D, D), jnp.bfloat16),
        ),
        in_specs=[hbm] * 6,
        out_specs=(hbm,) * 4,
        scratch_shapes=[
            pltpu.VMEM((STRIP, D), jnp.bfloat16),
            pltpu.VMEM((1, D), jnp.float32),
            pltpu.VMEM((1, D), jnp.float32),
            pltpu.VMEM((1, 3 * D), jnp.float32),
            pltpu.VMEM((2, CHUNKS, 4, CROWS, D), jnp.bfloat16),
            pltpu.VMEM((D, 2 * D), jnp.bfloat16),
            pltpu.VMEM((D, 2 * D), jnp.bfloat16),
            pltpu.VMEM((2, CHUNKS, 4, CROWS, 2 * D), jnp.bfloat16),
            pltpu.VMEM((STRIP, D), jnp.bfloat16),
            pltpu.SemaphoreType.DMA((STRIPS, CHUNKS)),
            pltpu.SemaphoreType.DMA((STRIPS, CHUNKS)),
            pltpu.SemaphoreType.DMA((2, 37)),
            pltpu.SemaphoreType.DMA((2, 37)),
            pltpu.SemaphoreType.DMA((7,)),
            pltpu.SemaphoreType.DMA((8, 4)),
            pltpu.SemaphoreType.DMA((8, 4)),
        ],
        compiler_params=pltpu.CompilerParams(
            collective_id=0, has_side_effects=True, vmem_limit_bytes=62 * 2**20),
    )(tokens, gain, beta, w_qkv, qkv_bias, w_out)


def attend_kernel(m_ref, q_hbm, k_hbm, v_hbm, tok_hbm, wo_hbm, bo_hbm, upd_ref, ctx_ref,
                  idx, k_ref, v_ref, qz, s_scr, mx, lsum, acc, q_ref, tok_ref, wo_ref, bo_ref, ksem, vsem, insem):
    def fetch(hbm, ref, sem, j):
        rows = pl.ds(pl.multiple_of(j * BLOCK, BLOCK), BLOCK)
        return pltpu.make_async_copy(hbm.at[rows], ref.at[rows], sem.at[j])

    def each(hbm, ref, sem, start):
        def body(j, c):
            @pl.when(m_ref[0, j] + m_ref[1, j] + m_ref[2, j] > 0)
            def _():
                copy = fetch(hbm, ref, sem, j)
                if start:
                    copy.start()
                else:
                    copy.wait()
            return c
        lax.fori_loop(0, NB, body, 0)

    fills = [pltpu.make_async_copy(source, target, insem.at[i]) for i, (source, target) in enumerate(
        ((q_hbm, q_ref), (wo_hbm, wo_ref), (tok_hbm, tok_ref), (bo_hbm, bo_ref)))]
    fills[0].start()
    each(k_hbm, k_ref, ksem, True)
    each(v_hbm, v_ref, vsem, True)
    for fill in fills[1:]:
        fill.start()
    fills[0].wait()
    lane = lax.broadcasted_iota(jnp.int32, (BLOCK, 128), 1)
    low = lane < 64
    for i in range(STRIP // BLOCK):
        def build(j, c):
            idx[c] = j
            return c + (m_ref[i, j] > 0).astype(jnp.int32)
        n = lax.fori_loop(0, NB, build, jnp.int32(0))
        idx[n] = idx[n - 1]
        steps = (n + 1) // 2
        for hp in range(PAIRS):
            qv = q_ref[i * BLOCK:(i + 1) * BLOCK, hp * 128:(hp + 1) * 128]
            zero = jnp.zeros_like(qv)
            qz[hp, :BLOCK] = jnp.where(low, qv, zero)
            qz[hp, BLOCK:] = jnp.where(low, zero, qv)
        mx[...] = jnp.full_like(mx, NEG_FILL)
        lsum[...] = jnp.zeros_like(lsum)
        acc[...] = jnp.zeros_like(acc)
        if i == 0:
            each(k_hbm, k_ref, ksem, False)

        def pass1(t, _):
            r0 = pl.multiple_of(idx[2 * t] * BLOCK, BLOCK)
            r1 = pl.multiple_of(idx[2 * t + 1] * BLOCK, BLOCK)
            for hp in range(PAIRS):
                ln = slice(hp * 128, (hp + 1) * 128)
                kk = jnp.concatenate([k_ref[pl.ds(r0, BLOCK), ln], k_ref[pl.ds(r1, BLOCK), ln]], axis=0)
                s = lax.dot_general(qz[hp], kk, (((1,), (1,)), ((), ())), preferred_element_type=jnp.float32)
                s_scr[t, hp] = s
                mx[hp] = jnp.maximum(mx[hp], jnp.maximum(s[:, :128], s[:, 128:]))
            return 0
        lax.fori_loop(0, steps, pass1, 0)

        @pl.when(lax.rem(n, 2) == 1)
        def _():
            for hp in range(PAIRS):
                s_scr[steps - 1, hp, :, 128:] = jnp.full((256, 128), NEG_FILL, jnp.float32)
        for hp in range(PAIRS):
            mx[hp] = jnp.broadcast_to(jnp.max(mx[hp], axis=1, keepdims=True), (256, 128))
        if i == 0:
            each(v_hbm, v_ref, vsem, False)

        def pass2(t, _):
            r0 = pl.multiple_of(idx[2 * t] * BLOCK, BLOCK)
            r1 = pl.multiple_of(idx[2 * t + 1] * BLOCK, BLOCK)
            for hp in range(PAIRS):
                ln = slice(hp * 128, (hp + 1) * 128)
                s = s_scr[t, hp]
                mm = mx[hp]
                p0 = jnp.exp(s[:, :128] - mm)
                p1 = jnp.exp(s[:, 128:] - mm)
                lsum[hp] += p0 + p1
                pb = jnp.concatenate([p0.astype(jnp.bfloat16), p1.astype(jnp.bfloat16)], axis=1)
                vv = jnp.concatenate([v_ref[pl.ds(r0, BLOCK), ln], v_ref[pl.ds(r1, BLOCK), ln]], axis=0)
                acc[hp] += jnp.dot(pb, vv, preferred_element_type=jnp.float32)
            return 0
        lax.fori_loop(0, steps, pass2, 0)
        rows = slice(i * BLOCK, (i + 1) * BLOCK)
        for hp in range(PAIRS):
            o = acc[hp] / jnp.sum(lsum[hp], axis=1, keepdims=True)
            ctx_ref[rows, hp * 128:(hp + 1) * 128] = jnp.where(low, o[:BLOCK], o[BLOCK:]).astype(jnp.bfloat16)
    for fill in fills[1:]:
        fill.wait()
    projected = jnp.dot(ctx_ref[...], wo_ref[...], preferred_element_type=jnp.float32)
    upd_ref[...] = (tok_ref[...].astype(jnp.float32) + projected + bo_ref[...]).astype(jnp.bfloat16)


def attention(masks, q, k, v, tokens, w_out, out_bias):
    vmem = pl.BlockSpec(memory_space=pltpu.VMEM)
    hbm = pl.BlockSpec(memory_space=pltpu.HBM)
    return pl.pallas_call(
        attend_kernel,
        name="attend",
        out_shape=(jax.ShapeDtypeStruct((STRIP, D), jnp.bfloat16),) * 2,
        in_specs=[pl.BlockSpec(memory_space=pltpu.SMEM)] + [hbm] * 6,
        out_specs=(vmem, vmem),
        scratch_shapes=[
            pltpu.SMEM((NB + 1,), jnp.int32),
            pltpu.VMEM((NB * BLOCK, D), jnp.bfloat16),
            pltpu.VMEM((NB * BLOCK, D), jnp.bfloat16),
            pltpu.VMEM((PAIRS, 256, 128), jnp.bfloat16),
            pltpu.VMEM((NB // 2, PAIRS, 256, 256), jnp.float32),
            pltpu.VMEM((PAIRS, 256, 128), jnp.float32),
            pltpu.VMEM((PAIRS, 256, 128), jnp.float32),
            pltpu.VMEM((PAIRS, 256, 128), jnp.float32),
            pltpu.VMEM((STRIP, D), jnp.bfloat16),
            pltpu.VMEM((STRIP, D), jnp.bfloat16),
            pltpu.VMEM((D, D), jnp.bfloat16),
            pltpu.VMEM((1, D), jnp.float32),
            pltpu.SemaphoreType.DMA((NB,)),
            pltpu.SemaphoreType.DMA((NB,)),
            pltpu.SemaphoreType.DMA((4,)),
        ],
        compiler_params=pltpu.CompilerParams(vmem_limit_bytes=62 * 2**20),
    )(masks, q, k, v, tokens, w_out, out_bias)


def on_device(tokens, masks, ln_gain, ln_bias, w_qkv, qkv_bias, w_out, out_bias):
    sheet = tokens[0]
    q, k, v, w_full = gather(sheet, ln_gain[None], ln_bias[None], w_qkv, qkv_bias[None], w_out)
    k, v = (array.reshape(STRIPS * STRIP, D) for array in (k, v))
    updated, context = attention(masks[0], q, k, v, sheet, w_full, out_bias[None])
    return (updated[None], context[None])


def solution(mesh):
    placed = (
        P("dp", "seq", None),
        P("dp", "seq", None),
        P(),
        P(),
        P("dp", None),
        P(),
        P("dp", None),
        P(),
    )
    return jax.shard_map(
        on_device,
        mesh=mesh,
        in_specs=placed,
        out_specs=(P("dp", "seq", None), P("dp", "seq", None)),
        check_vma=False,
    )
```

```python
import jax
import jax.numpy as jnp
from jax import lax
from jax.experimental import pallas as pl
from jax.experimental.pallas import tpu as pltpu
from jax.sharding import PartitionSpec as P

D = 1024
HEADS = 16
BLOCK = 128
NB = 24
STRIP = 384
STRIPS = 8
ROWS = 32
PAIRS = 8
CHUNKS = 8
AHEAD = 4
CROSSING = 2
CROWS = STRIP // CHUNKS

NEG_FILL = -1e30
EPSILON = 1e-06
MESH = pl.DeviceIdType.MESH

SELF, BEFORE, AFTER, ACROSS = range(4)


def gather_kernel(tok_hbm, gain_hbm, beta_hbm, wq_hbm, bq_hbm, wo_hbm,
                  q_hbm, k_hbm, v_hbm, wo_out,
                  tok_ref, gain_ref, beta_ref, bq_ref, toks, w_all, w_two, staged, q_ref,
                  tsend, trecv, wsend, wrecv, insem, ksem, vsem):
    dp = lax.axis_index("dp")
    sq = lax.axis_index("seq")
    core = lax.rem(dp, 2)
    x = lax.rem(dp // 2, 4)
    zl = dp // 8
    y = lax.rem(sq, 4)
    zh = sq // 4
    z = zh * 4 + zl

    def device(dx=0, dy=0, dz=0, flip=False):
        zz = lax.rem(z + dz + 8, 8)
        cc = 1 - core if flip else core
        return (lax.rem(zz, 4) * 8 + lax.rem(x + dx + 4, 4) * 2 + cc,
                (zz // 4) * 4 + lax.rem(y + dy + 4, 4))

    own_rows = pl.ds(pl.multiple_of(dp * ROWS, ROWS), ROWS)
    fills = [
        pltpu.make_async_copy(source, target, insem.at[i])
        for i, (source, target) in enumerate((
            (wq_hbm.at[:, D:], w_all.at[own_rows]), (tok_hbm, tok_ref), (wq_hbm.at[:, :D], w_two.at[own_rows, :D]),
            (wo_hbm, w_two.at[own_rows, D:]),
            (gain_hbm, gain_ref), (beta_hbm, beta_ref), (bq_hbm, bq_ref)))]
    for fill in fills:
        fill.start()

    partners = [device(dx=1), device(dx=-1), device(dy=1), device(dy=-1), device(dz=1), device(dz=-1),
                device(dz=2), device(dz=-2), device(dz=4), device(flip=True)]
    barrier = pltpu.get_barrier_semaphore()
    for partner in partners:
        pl.semaphore_signal(barrier, inc=1, device_id=partner, device_id_type=MESH)
    for fill in fills:
        fill.wait()
    pl.semaphore_wait(barrier, len(partners))

    def token_copy(plane, place, chunk):
        source = plane, SELF
        if place == SELF:
            source, target = (0, SELF), device(dz=4)
        elif place == BEFORE:
            target = device(dy=1)
        elif place == AFTER:
            target = device(dy=-1)
        elif chunk % 2 == 0:
            source, target = (plane, BEFORE), device(dy=1)
        else:
            source, target = (plane, AFTER), device(dy=-1)
        slot = plane * 4 + place
        return pltpu.make_async_remote_copy(
            src_ref=toks.at[source[0], chunk, source[1]], dst_ref=toks.at[plane, chunk, place],
            send_sem=tsend.at[slot, chunk], recv_sem=trecv.at[slot, chunk],
            device_id=target, device_id_type=MESH)

    weights = (w_all, w_two)

    def shard(k, dx):
        return lax.rem(zl + (0, 3, 1, 2)[k], 4) * 8 + lax.rem(x + dx + 4, 4) * 2 + core

    def weight_copy(which, name, k=0, place=SELF):
        ref = weights[which]
        first, count = 0, ROWS
        if name == "z":
            owner, index = shard(0, 0), k
            target = device(dz=(0, 1, -1, 2, -2)[k])
            if k >= 3:
                first, count = (k - 3) * (ROWS // 2), ROWS // 2
        elif name == "x":
            index = 5 + k * 4 + place
            if place == BEFORE:
                owner, target = shard(k, 0), device(dx=1)
            elif place == AFTER:
                owner, target = shard(k, 0), device(dx=-1)
            elif place == SELF:
                owner, target = shard(k, -1), device(dx=1)
                count = ROWS // 2
            else:
                owner, target = shard(k, 1), device(dx=-1)
                first, count = ROWS // 2, ROWS // 2
        else:
            index = 21 + k * 4 + place
            owner, target = shard(k, (0, -1, 1, 2)[place]), device(flip=True)
        rows = pl.ds(pl.multiple_of(owner * ROWS + first, ROWS // 2), count)
        return pltpu.make_async_remote_copy(
            src_ref=ref.at[rows], dst_ref=ref.at[rows],
            send_sem=wsend.at[which, index], recv_sem=wrecv.at[which, index],
            device_id=target, device_id_type=MESH)

    sent = []

    def go(copy):
        copy.start()
        sent.append(copy)

    def arrive(copy):
        copy.wait_recv()

    def spread(which, k):
        go(weight_copy(which, "x", k, BEFORE))
        go(weight_copy(which, "x", k, AFTER))
        go(weight_copy(which, "c", k, SELF))

    def around(which):
        for k in (1, 2, 3, 4):
            go(weight_copy(which, "z", k))

    def z_arrived(which, k):
        arrive(weight_copy(which, "z", k))
        if k == 3:
            arrive(weight_copy(which, "z", 4))
        spread(which, k)

    def x_arrived(which, k):
        arrive(weight_copy(which, "x", k, BEFORE))
        go(weight_copy(which, "x", k, SELF))
        go(weight_copy(which, "c", k, BEFORE))
        arrive(weight_copy(which, "x", k, AFTER))
        go(weight_copy(which, "x", k, ACROSS))
        go(weight_copy(which, "c", k, AFTER))

    def x_across(which, k):
        arrive(weight_copy(which, "x", k, SELF))
        arrive(weight_copy(which, "x", k, ACROSS))
        go(weight_copy(which, "c", k, ACROSS))

    def core_arrived(which):
        for k in range(4):
            for place in range(4):
                arrive(weight_copy(which, "c", k, place))

    def normalize(chunk):
        rows = pl.ds(chunk * CROWS, CROWS)
        values = tok_ref[rows, :].astype(jnp.float32)
        center = jnp.mean(values, axis=-1, keepdims=True)
        moved = values - center
        spread_ = jnp.mean(jnp.square(moved), axis=-1, keepdims=True)
        normed = moved * lax.rsqrt(spread_ + EPSILON)
        toks[0, chunk, SELF] = (normed * gain_ref[...] + beta_ref[...]).astype(jnp.bfloat16)

    def offer(plane, chunk):
        if chunk < CHUNKS:
            go(token_copy(plane, BEFORE, chunk))
            go(token_copy(plane, AFTER, chunk))

    def start():
        for chunk in range(CHUNKS):
            normalize(chunk)
            if chunk < AHEAD:
                offer(0, chunk)

    def cross(chunk):
        if chunk < CHUNKS:
            go(token_copy(1, SELF, chunk))

    def step(plane, chunk):
        first, second = (BEFORE, AFTER) if chunk % 2 == 0 else (AFTER, BEFORE)
        arrive(token_copy(plane, first, chunk))
        go(token_copy(plane, ACROSS, chunk))
        if plane == 0:
            offer(plane, chunk + AHEAD)
        arrive(token_copy(plane, second, chunk))

    def crossed(chunk):
        arrive(token_copy(1, SELF, chunk))
        cross(chunk + CROSSING)
        offer(1, chunk)

    def across(plane, chunks):
        for chunk in chunks:
            arrive(token_copy(plane, ACROSS, chunk))

    written = []

    def project(plane, first, end, piece):
        count = (end - first) * 4 * CROWS
        read = toks[plane, first:end].reshape(count, D)
        half = zh if plane == 0 else 1 - zh
        for lane, out, sem in ((0, k_hbm, ksem), (D, v_hbm, vsem)):
            made = jnp.dot(read, w_all[:, lane:D + lane], preferred_element_type=jnp.float32)
            made = (made + bq_ref[:, D + lane:2 * D + lane]).astype(jnp.bfloat16)
            staged[plane, first:end, :, :, lane:lane + D] = made.reshape(end - first, 4, CROWS, D)
            for place in range(4):
                strip = half * 4 + lax.rem(y + (0, 3, 1, 2)[place], 4)
                copy = pltpu.make_async_copy(
                    staged.at[plane, first:end, place, :, lane:lane + D], out.at[strip, first:end], sem.at[piece, place])
                copy.start()
                written.append(copy)

    def queries():
        own = toks[0, :, SELF].reshape(STRIP, D)
        made = jnp.dot(own, w_two[:, :D], preferred_element_type=jnp.float32)
        q_ref[...] = (made + bq_ref[:, :D]).astype(jnp.bfloat16) * jnp.bfloat16(0.125)
        copy = pltpu.make_async_copy(q_ref, q_hbm, insem.at[0])
        copy.start()
        written.append(copy)

    def output_weights():
        copy = pltpu.make_async_copy(w_two.at[:, D:], wo_out, insem.at[1])
        copy.start()
        written.append(copy)

    around(0)
    spread(0, 0)
    start()
    cross(0)
    step(0, 0)
    x_arrived(0, 0)
    step(0, 1)
    x_across(0, 0)
    z_arrived(0, 1)
    z_arrived(0, 2)
    z_arrived(0, 3)
    around(1)
    cross(1)
    step(0, 2)
    crossed(0)
    step(0, 3)
    step(0, 4)
    x_arrived(0, 1)
    x_arrived(0, 2)
    x_arrived(0, 3)
    spread(1, 0)
    step(0, 5)
    x_across(0, 1)
    x_across(0, 2)
    x_across(0, 3)
    z_arrived(1, 1)
    z_arrived(1, 2)
    z_arrived(1, 3)
    step(0, 6)
    crossed(1)
    core_arrived(0)
    x_arrived(1, 0)
    step(0, 7)
    across(0, range(CHUNKS))
    project(0, 0, 2, 0)
    crossed(2)
    step(1, 0)
    project(0, 2, 4, 1)
    x_arrived(1, 1)
    x_arrived(1, 2)
    x_arrived(1, 3)
    x_across(1, 0)
    crossed(3)
    step(1, 1)
    project(0, 4, 6, 2)
    crossed(4)
    step(1, 2)
    x_across(1, 1)
    x_across(1, 2)
    x_across(1, 3)
    project(0, 6, 8, 3)
    crossed(5)
    step(1, 3)
    across(1, (0, 1))
    project(1, 0, 2, 4)
    core_arrived(1)
    queries()
    crossed(6)
    step(1, 4)
    across(1, (2, 3))
    project(1, 2, 4, 5)
    crossed(7)
    step(1, 5)
    output_weights()
    step(1, 6)
    across(1, (4, 5, 6))
    project(1, 4, 7, 6)
    step(1, 7)
    across(1, (7,))
    project(1, 7, 8, 7)
    for copy in written:
        copy.wait()
    for copy in sent:
        copy.wait_send()


def gather(tokens, gain, beta, w_qkv, qkv_bias, w_out):
    hbm = pl.BlockSpec(memory_space=pltpu.HBM)
    return pl.pallas_call(
        gather_kernel,
        name="gather_and_project",
        out_shape=(
            jax.ShapeDtypeStruct((STRIP, D), jnp.bfloat16),
            jax.ShapeDtypeStruct((STRIPS, CHUNKS, CROWS, D), jnp.bfloat16),
            jax.ShapeDtypeStruct((STRIPS, CHUNKS, CROWS, D), jnp.bfloat16),
            jax.ShapeDtypeStruct((D, D), jnp.bfloat16),
        ),
        in_specs=[hbm] * 6,
        out_specs=(hbm,) * 4,
        scratch_shapes=[
            pltpu.VMEM((STRIP, D), jnp.bfloat16),
            pltpu.VMEM((1, D), jnp.float32),
            pltpu.VMEM((1, D), jnp.float32),
            pltpu.VMEM((1, 3 * D), jnp.float32),
            pltpu.VMEM((2, CHUNKS, 4, CROWS, D), jnp.bfloat16),
            pltpu.VMEM((D, 2 * D), jnp.bfloat16),
            pltpu.VMEM((D, 2 * D), jnp.bfloat16),
            pltpu.VMEM((2, CHUNKS, 4, CROWS, 2 * D), jnp.bfloat16),
            pltpu.VMEM((STRIP, D), jnp.bfloat16),
            pltpu.SemaphoreType.DMA((STRIPS, CHUNKS)),
            pltpu.SemaphoreType.DMA((STRIPS, CHUNKS)),
            pltpu.SemaphoreType.DMA((2, 37)),
            pltpu.SemaphoreType.DMA((2, 37)),
            pltpu.SemaphoreType.DMA((7,)),
            pltpu.SemaphoreType.DMA((8, 4)),
            pltpu.SemaphoreType.DMA((8, 4)),
        ],
        compiler_params=pltpu.CompilerParams(
            collective_id=0, has_side_effects=True, vmem_limit_bytes=62 * 2**20),
    )(tokens, gain, beta, w_qkv, qkv_bias, w_out)


def attend_kernel(m_ref, q_hbm, k_hbm, v_hbm, tok_hbm, wo_hbm, bo_hbm, upd_ref, ctx_ref,
                  idx, k_ref, v_ref, qz, s_scr, mx, lsum, acc, q_ref, tok_ref, wo_ref, bo_ref, ksem, vsem, insem):
    def fetch(hbm, ref, sem, j):
        rows = pl.ds(pl.multiple_of(j * BLOCK, BLOCK), BLOCK)
        return pltpu.make_async_copy(hbm.at[rows], ref.at[rows], sem.at[j])

    def each(hbm, ref, sem, start):
        def body(j, c):
            @pl.when(m_ref[0, j] + m_ref[1, j] + m_ref[2, j] > 0)
            def _():
                copy = fetch(hbm, ref, sem, j)
                if start:
                    copy.start()
                else:
                    copy.wait()
            return c
        lax.fori_loop(0, NB, body, 0)

    fills = [pltpu.make_async_copy(source, target, insem.at[i]) for i, (source, target) in enumerate(
        ((q_hbm, q_ref), (wo_hbm, wo_ref), (tok_hbm, tok_ref), (bo_hbm, bo_ref)))]
    fills[0].start()
    each(k_hbm, k_ref, ksem, True)
    each(v_hbm, v_ref, vsem, True)
    for fill in fills[1:]:
        fill.start()
    fills[0].wait()
    lane = lax.broadcasted_iota(jnp.int32, (BLOCK, 128), 1)
    low = lane < 64
    for i in range(STRIP // BLOCK):
        def build(j, c):
            idx[c] = j
            return c + (m_ref[i, j] > 0).astype(jnp.int32)
        n = lax.fori_loop(0, NB, build, jnp.int32(0))
        idx[n] = idx[n - 1]
        steps = (n + 1) // 2
        for hp in range(PAIRS):
            qv = q_ref[i * BLOCK:(i + 1) * BLOCK, hp * 128:(hp + 1) * 128]
            zero = jnp.zeros_like(qv)
            qz[hp, :BLOCK] = jnp.where(low, qv, zero)
            qz[hp, BLOCK:] = jnp.where(low, zero, qv)
        mx[...] = jnp.full_like(mx, NEG_FILL)
        lsum[...] = jnp.zeros_like(lsum)
        acc[...] = jnp.zeros_like(acc)
        if i == 0:
            each(k_hbm, k_ref, ksem, False)

        def pass1(t, _):
            r0 = pl.multiple_of(idx[2 * t] * BLOCK, BLOCK)
            r1 = pl.multiple_of(idx[2 * t + 1] * BLOCK, BLOCK)
            for hp in range(PAIRS):
                ln = slice(hp * 128, (hp + 1) * 128)
                kk = jnp.concatenate([k_ref[pl.ds(r0, BLOCK), ln], k_ref[pl.ds(r1, BLOCK), ln]], axis=0)
                s = lax.dot_general(qz[hp], kk, (((1,), (1,)), ((), ())), preferred_element_type=jnp.float32)
                s_scr[t, hp] = s
                mx[hp] = jnp.maximum(mx[hp], jnp.maximum(s[:, :128], s[:, 128:]))
            return 0
        lax.fori_loop(0, steps, pass1, 0)

        @pl.when(lax.rem(n, 2) == 1)
        def _():
            for hp in range(PAIRS):
                s_scr[steps - 1, hp, :, 128:] = jnp.full((256, 128), NEG_FILL, jnp.float32)
        for hp in range(PAIRS):
            mx[hp] = jnp.broadcast_to(jnp.max(mx[hp], axis=1, keepdims=True), (256, 128))
        if i == 0:
            each(v_hbm, v_ref, vsem, False)

        def pass2(t, _):
            r0 = pl.multiple_of(idx[2 * t] * BLOCK, BLOCK)
            r1 = pl.multiple_of(idx[2 * t + 1] * BLOCK, BLOCK)
            for hp in range(PAIRS):
                ln = slice(hp * 128, (hp + 1) * 128)
                s = s_scr[t, hp]
                mm = mx[hp]
                p0 = jnp.exp(s[:, :128] - mm)
                p1 = jnp.exp(s[:, 128:] - mm)
                lsum[hp] += p0 + p1
                pb = jnp.concatenate([p0.astype(jnp.bfloat16), p1.astype(jnp.bfloat16)], axis=1)
                vv = jnp.concatenate([v_ref[pl.ds(r0, BLOCK), ln], v_ref[pl.ds(r1, BLOCK), ln]], axis=0)
                acc[hp] += jnp.dot(pb, vv, preferred_element_type=jnp.float32)
            return 0
        lax.fori_loop(0, steps, pass2, 0)
        rows = slice(i * BLOCK, (i + 1) * BLOCK)
        for hp in range(PAIRS):
            o = acc[hp] / jnp.sum(lsum[hp], axis=1, keepdims=True)
            ctx_ref[rows, hp * 128:(hp + 1) * 128] = jnp.where(low, o[:BLOCK], o[BLOCK:]).astype(jnp.bfloat16)
    for fill in fills[1:]:
        fill.wait()
    projected = jnp.dot(ctx_ref[...], wo_ref[...], preferred_element_type=jnp.float32)
    upd_ref[...] = (tok_ref[...].astype(jnp.float32) + projected + bo_ref[...]).astype(jnp.bfloat16)


def attention(masks, q, k, v, tokens, w_out, out_bias):
    vmem = pl.BlockSpec(memory_space=pltpu.VMEM)
    hbm = pl.BlockSpec(memory_space=pltpu.HBM)
    return pl.pallas_call(
        attend_kernel,
        name="attend",
        out_shape=(jax.ShapeDtypeStruct((STRIP, D), jnp.bfloat16),) * 2,
        in_specs=[pl.BlockSpec(memory_space=pltpu.SMEM)] + [hbm] * 6,
        out_specs=(vmem, vmem),
        scratch_shapes=[
            pltpu.SMEM((NB + 1,), jnp.int32),
            pltpu.VMEM((NB * BLOCK, D), jnp.bfloat16),
            pltpu.VMEM((NB * BLOCK, D), jnp.bfloat16),
            pltpu.VMEM((PAIRS, 256, 128), jnp.bfloat16),
            pltpu.VMEM((NB // 2, PAIRS, 256, 256), jnp.float32),
            pltpu.VMEM((PAIRS, 256, 128), jnp.float32),
            pltpu.VMEM((PAIRS, 256, 128), jnp.float32),
            pltpu.VMEM((PAIRS, 256, 128), jnp.float32),
            pltpu.VMEM((STRIP, D), jnp.bfloat16),
            pltpu.VMEM((STRIP, D), jnp.bfloat16),
            pltpu.VMEM((D, D), jnp.bfloat16),
            pltpu.VMEM((1, D), jnp.float32),
            pltpu.SemaphoreType.DMA((NB,)),
            pltpu.SemaphoreType.DMA((NB,)),
            pltpu.SemaphoreType.DMA((4,)),
        ],
        compiler_params=pltpu.CompilerParams(vmem_limit_bytes=62 * 2**20),
    )(masks, q, k, v, tokens, w_out, out_bias)


def on_device(tokens, masks, ln_gain, ln_bias, w_qkv, qkv_bias, w_out, out_bias):
    sheet = tokens[0]
    q, k, v, w_full = gather(sheet, ln_gain[None], ln_bias[None], w_qkv, qkv_bias[None], w_out)
    k, v = (array.reshape(STRIPS * STRIP, D) for array in (k, v))
    updated, context = attention(masks[0], q, k, v, sheet, w_full, out_bias[None])
    return (updated[None], context[None])


def solution(mesh):
    placed = (
        P("dp", "seq", None),
        P("dp", "seq", None),
        P(),
        P(),
        P("dp", None),
        P(),
        P("dp", None),
        P(),
    )
    return jax.shard_map(
        on_device,
        mesh=mesh,
        in_specs=placed,
        out_specs=(P("dp", "seq", None), P("dp", "seq", None)),
        check_vma=False,
    )
```
